32 devices in a mesh: cfg: 4 (over z), mode: 8 (over y, x, core).
Axes of the slice: x: 2, y: 2, z: 4, core: 2. Of those that a mesh axis runs over, the one named last changes fastest.
Arguments:
- coords: bfloat16 [10368, 2048], P('mode', 'cfg'), may hold values from -6 to 6
- curvature: float32 [10368], P('mode'), may hold values from 0.2 to 5
- weight: float32 [10368], P('mode'), may hold values from 0.3 to 3
- polar: bfloat16 [10368, 10368], P('mode'), may hold values from -0.078125 to 0.078125
- forces: bfloat16 [10368, 2048], P('mode', 'cfg'), may hold values from -6 to 6
Outputs:
- gradient: float32 [10368, 10368], P('cfg', 'mode')
The draws below stay inside these ranges and needn't reach their ends.
All inputs are finite; a program needn't handle non-finite values.
Results may differ from the reference program's by a relative error of at most 0.019.
Values may be sent and summed in bfloat16 or wider, within the bound.
A program may use at most 192 MiB of HBM per device.

```python
import math
import jax
import jax.numpy as jnp
from jax import lax

M = 10368
CFG_DEV = 512
CONFIGS = 2048
N_CFG = 4
N_MODE = 8


def with_spikes(values, key, source, target, blocks, factor):
    owner, partner = [(jnp.arange(values.shape[dim]) // (values.shape[dim] // blocks)).reshape([-1 if axis == dim else 1 for axis in range(values.ndim)]) for dim in (source, target)]
    chosen = jax.random.permutation(key, blocks)[partner]
    strong = (owner == chosen) | (owner == (partner + blocks // 2) % blocks)
    return jnp.where(strong, factor * values, values)


def block_scale(rng, extent, cuts, least, top_value):
    factor_of, own = 1.0, jax.random.fold_in(rng, 6)
    for dim, blocks in cuts:
        heights = jnp.exp(jax.random.uniform(jax.random.fold_in(own, dim), (blocks,), jnp.float32, least / len(cuts), top_value / len(cuts)))
        factor_of = factor_of * jnp.repeat(heights, extent[dim] // blocks).reshape([-1 if axis == dim else 1 for axis in range(len(extent))])
    return factor_of


def normal_values(own_key, dims, width, bound, cuts=(), held_as=jnp.bfloat16):
    loudness = block_scale(own_key, dims, cuts, -0.22, 0.18) if cuts else 1.0
    entries = jax.random.normal(own_key, dims, jnp.float32) * width * loudness
    return jnp.minimum(jnp.maximum(entries, -bound), bound).astype(held_as)


def noise_with(key, shape, deviation, limit, cuts, heavy, dtype=jnp.bfloat16):
    entries = deviation * jax.random.normal(key, shape, jnp.float32)
    if cuts:
        entries = entries * block_scale(key, shape, cuts, -0.22, 0.18)
    return jnp.clip(with_spikes(entries, jax.random.fold_in(key, 3), *heavy), -limit, limit).astype(dtype)


def setup_inputs(seed: int = 0) -> dict:
    key_list = jax.random.split(jax.random.key(seed), 6)
    return {
        "coords": normal_values(key_list[0], (M, CONFIGS), 1.0, 6.0, ((0, 8), (1, 4))),
        "curvature": jnp.clip(jnp.exp(math.log(5.0) - 3.218876 * jax.random.uniform(key_list[1], (M,), jnp.float32) ** block_scale(key_list[1], (M,), ((0, 8),), -0.2, 0.2)), 0.2, 5.0),
        "weight": jnp.clip(jnp.exp(math.log(3.0) - 2.3025851 * jax.random.uniform(key_list[2], (M,), jnp.float32) ** block_scale(key_list[2], (M,), ((0, 8),), -0.2, 0.2)), 0.3, 3.0),
        "polar": noise_with(key_list[3], (M, M), M ** -0.5, 0.078125, ((0, 8),), (0, 1, 8, 2.0)),
        "forces": normal_values(key_list[4], (M, CONFIGS), 1.0, 6.0, ((0, 8), (1, 4))),
    }


def reference(coords, curvature, weight, polar, forces):
    f32 = jnp.float32
    bf16 = jnp.bfloat16
    block_modes = M // N_MODE
    scaled = (coords.astype(f32) * curvature[:, None]).astype(bf16)
    weighted = (coords.astype(f32) * weight[:, None]).astype(bf16)
    scaled_blocks = scaled.reshape(N_MODE, block_modes, CONFIGS)
    polar_blocks = polar.reshape(N_MODE, block_modes, M)

    def harmonic_step(total, pieces):
        scaled_piece, polar_piece = pieces
        term = jnp.dot(polar_piece.astype(f32).T, scaled_piece.astype(f32))
        rounded = lax.optimization_barrier(term.astype(bf16))
        return (total + rounded.astype(f32), 0)
    harmonic, unused = lax.scan(harmonic_step, jnp.zeros((M, CONFIGS), f32), (scaled_blocks, polar_blocks))
    residual = (forces.astype(f32) + harmonic).astype(bf16)
    factor = 1.0 / math.sqrt(CONFIGS)
    resid_blocks = residual.reshape(M, N_CFG, CFG_DEV).transpose(1, 0, 2)
    weight_blocks = weighted.reshape(M, N_CFG, CFG_DEV).transpose(1, 0, 2)

    def gradient_step(total, pieces):
        resid_piece, weight_piece = pieces
        term = jnp.dot(resid_piece.astype(f32), weight_piece.astype(f32).T) * factor
        rounded = lax.optimization_barrier(term.astype(bf16))
        return (total + rounded.astype(f32), 0)
    gradient, unused_two = lax.scan(gradient_step, jnp.zeros((M, M), f32), (resid_blocks, weight_blocks))
    return gradient
```

```python
import functools
import math

import jax
import jax.numpy as jnp
from jax import lax
from jax.experimental import pallas as pl
from jax.experimental.pallas import tpu as pltpu
from jax.sharding import PartitionSpec as P


def tile_of(extent, most):
    return max(t for t in range(8, most + 1, 8) if extent % t == 0)


def exchange_kernel(n, axis, step, whole, relative, x_ref, out_ref, send, recv, own):
    me = lax.axis_index(axis)
    here, rest = me // step, lax.rem(me, step)
    barrier = pltpu.get_barrier_semaphore()
    for d in range(1, n):
        target = lax.rem(here + d, n) * step + rest
        pl.semaphore_signal(
            barrier, inc=1, device_id={axis: target}, device_id_type=pl.DeviceIdType.MESH
        )
    pl.semaphore_wait(barrier, n - 1)
    copies = []
    for d in range(1, n):
        place = lax.rem(here + d, n)
        copies.append(
            pltpu.make_async_remote_copy(
                src_ref=x_ref if whole else x_ref.at[place],
                dst_ref=out_ref.at[n - d if relative else here],
                send_sem=send.at[d - 1],
                recv_sem=recv.at[d - 1],
                device_id={axis: place * step + rest},
                device_id_type=pl.DeviceIdType.MESH,
            )
        )
    local = pltpu.make_async_copy(
        x_ref if whole else x_ref.at[here], out_ref.at[0 if relative else here], own
    )
    for copy in copies:
        copy.start()
    local.start()
    local.wait()
    for copy in copies:
        copy.wait()


def exchange(x, axis, n, step, whole, relative, number):
    slab = x.shape if whole else x.shape[1:]
    return pl.pallas_call(
        functools.partial(exchange_kernel, n, axis, step, whole, relative),
        out_shape=jax.ShapeDtypeStruct((n, *slab), x.dtype),
        in_specs=[pl.BlockSpec(memory_space=pltpu.VMEM)],
        out_specs=pl.BlockSpec(memory_space=pl.ANY),
        scratch_shapes=[
            pltpu.SemaphoreType.DMA((n - 1,)),
            pltpu.SemaphoreType.DMA((n - 1,)),
            pltpu.SemaphoreType.DMA,
        ],
        cost_estimate=pl.CostEstimate(flops=0, bytes_accessed=150_000_000, transcendentals=0),
        compiler_params=pltpu.CompilerParams(
            collective_id=number, has_side_effects=True, vmem_limit_bytes=16 * 1024 * 1024
        ),
    )(x)


def share_kernel(scaled, polar, out):
    block = lax.dot_general(
        scaled[...], polar[...], (((1,), (0,)), ((), ())), preferred_element_type=jnp.float32
    ).astype(out.dtype)
    width = out.shape[2]
    for q in range(out.shape[0]):
        out[q] = block[q * width : (q + 1) * width].T


def share(scaled, polar, n):
    configs_dev, rows = scaled.shape
    whole = polar.shape[1]
    tile = max(t for t in range(128, 1153, 128) if whole % t == 0)
    return pl.pallas_call(
        share_kernel,
        grid=(whole // tile,),
        out_shape=jax.ShapeDtypeStruct((n, whole, configs_dev // n), polar.dtype),
        in_specs=[
            pl.BlockSpec((configs_dev, rows), lambda i: (0, 0)),
            pl.BlockSpec((rows, tile), lambda i: (0, i)),
        ],
        out_specs=pl.BlockSpec((n, tile, configs_dev // n), lambda i: (0, i, 0)),
        compiler_params=pltpu.CompilerParams(vmem_limit_bytes=40 * 1024 * 1024),
    )(scaled, polar)


def product_kernel(factor, per, resid, weights, out):
    across = (((1,), (1,)), ((), ()))
    n_mode, n, rows, _ = resid.shape
    for h in range(per):
        total = 0.0
        for d in range(n):
            block = jnp.concatenate([resid[j, d] for j in range(h, n_mode, per)], axis=1)
            total = total + lax.dot_general(
                weights[d], block, across, preferred_element_type=jnp.float32
            )
        out[:, h * rows : (h + 1) * rows] = total * factor


def product(resid, weights, per, factor):
    n_mode, n, rows, width = resid.shape
    cols, configs_dev = weights.shape[1:]
    tile = tile_of(cols, 224)
    return pl.pallas_call(
        functools.partial(product_kernel, factor, per),
        grid=(cols // tile,),
        out_shape=jax.ShapeDtypeStruct((cols, per * rows), jnp.float32),
        in_specs=[
            pl.BlockSpec((n_mode, n, rows, width), lambda i: (0, 0, 0, 0)),
            pl.BlockSpec((n, tile, configs_dev), lambda i: (0, i, 0)),
        ],
        out_specs=pl.BlockSpec((tile, per * rows), lambda i: (i, 0)),
        compiler_params=pltpu.CompilerParams(vmem_limit_bytes=56 * 1024 * 1024),
    )(resid, weights)


def on_device(coords, curvature, weight, polar, forces):
    f32 = jnp.float32
    bf16 = jnp.bfloat16
    n_cfg, n_mode = lax.axis_size("cfg"), lax.axis_size("mode")
    per = n_mode // n_cfg
    rows, configs_dev = coords.shape
    width = configs_dev // n_cfg
    factor = 1.0 / math.sqrt(configs_dev * n_cfg)
    scaled = (coords.astype(f32) * curvature[:, None]).astype(bf16)
    weighted = (coords.astype(f32) * weight[:, None]).astype(bf16)
    part = share(scaled.T, polar, n_cfg)
    part = part.reshape(n_cfg, n_cfg, per, rows, width).transpose(0, 2, 1, 3, 4)
    part = part.reshape(n_mode * n_cfg * rows, width)
    part, weighted, forces = lax.optimization_barrier((part, weighted, forces))
    shares = lax.psum_scatter(
        part, "mode", scatter_dimension=0, tiled=True
    ).reshape(n_cfg, rows, width)
    weights = exchange(weighted, "cfg", n_cfg, 1, True, True, 0)
    pushes = exchange(
        forces.reshape(rows, n_cfg, width).transpose(1, 0, 2), "mode", n_cfg, per, False, False, 1
    )
    pushes, weights = lax.optimization_barrier((pushes, weights))
    mine = (pushes.astype(f32) + shares.astype(f32)).astype(bf16)
    mine = exchange(mine, "cfg", n_cfg, 1, False, True, 2)
    resid = lax.all_gather(
        mine.reshape(n_cfg * rows, width), "mode", axis=0, tiled=True
    ).reshape(n_mode, n_cfg, rows, width)
    return product(resid, weights, per, factor).T


def solution(mesh):
    placed = (P("mode", "cfg"), P("mode"), P("mode"), P("mode", None), P("mode", "cfg"))
    return jax.shard_map(
        on_device, mesh=mesh, in_specs=placed, out_specs=P("cfg", "mode"), check_vma=False
    )
```

```python
import functools
import math

import jax
import jax.numpy as jnp
from jax import lax
from jax.experimental import pallas as pl
from jax.experimental.pallas import tpu as pltpu
from jax.sharding import PartitionSpec as P


def tile_of(extent, most):
    return max(t for t in range(8, most + 1, 8) if extent % t == 0)


def exchange_kernel(n, axis, step, whole, relative, x_ref, out_ref, send, recv, own):
    me = lax.axis_index(axis)
    here, rest = me // step, lax.rem(me, step)
    barrier = pltpu.get_barrier_semaphore()
    for d in range(1, n):
        target = lax.rem(here + d, n) * step + rest
        pl.semaphore_signal(
            barrier, inc=1, device_id={axis: target}, device_id_type=pl.DeviceIdType.MESH
        )
    pl.semaphore_wait(barrier, n - 1)
    copies = []
    for d in range(1, n):
        place = lax.rem(here + d, n)
        copies.append(
            pltpu.make_async_remote_copy(
                src_ref=x_ref if whole else x_ref.at[place],
                dst_ref=out_ref.at[n - d if relative else here],
                send_sem=send.at[d - 1],
                recv_sem=recv.at[d - 1],
                device_id={axis: place * step + rest},
                device_id_type=pl.DeviceIdType.MESH,
            )
        )
    local = pltpu.make_async_copy(
        x_ref if whole else x_ref.at[here], out_ref.at[0 if relative else here], own
    )
    for copy in copies:
        copy.start()
    local.start()
    local.wait()
    for copy in copies:
        copy.wait()


def exchange(x, axis, n, step, whole, relative, number):
    slab = x.shape if whole else x.shape[1:]
    return pl.pallas_call(
        functools.partial(exchange_kernel, n, axis, step, whole, relative),
        out_shape=jax.ShapeDtypeStruct((n, *slab), x.dtype),
        in_specs=[pl.BlockSpec(memory_space=pltpu.VMEM)],
        out_specs=pl.BlockSpec(memory_space=pl.ANY),
        scratch_shapes=[
            pltpu.SemaphoreType.DMA((n - 1,)),
            pltpu.SemaphoreType.DMA((n - 1,)),
            pltpu.SemaphoreType.DMA,
        ],
        cost_estimate=pl.CostEstimate(flops=0, bytes_accessed=150_000_000, transcendentals=0),
        compiler_params=pltpu.CompilerParams(
            collective_id=number, has_side_effects=True, vmem_limit_bytes=16 * 1024 * 1024
        ),
    )(x)


def share_kernel(scaled, polar, out):
    block = lax.dot_general(
        scaled[...], polar[...], (((1,), (0,)), ((), ())), preferred_element_type=jnp.float32
    ).astype(out.dtype)
    width = out.shape[2]
    for q in range(out.shape[0]):
        out[q] = block[q * width : (q + 1) * width].T


def share(scaled, polar, n):
    configs_dev, rows = scaled.shape
    whole = polar.shape[1]
    tile = max(t for t in range(128, 1153, 128) if whole % t == 0)
    return pl.pallas_call(
        share_kernel,
        grid=(whole // tile,),
        out_shape=jax.ShapeDtypeStruct((n, whole, configs_dev // n), polar.dtype),
        in_specs=[
            pl.BlockSpec((configs_dev, rows), lambda i: (0, 0)),
            pl.BlockSpec((rows, tile), lambda i: (0, i)),
        ],
        out_specs=pl.BlockSpec((n, tile, configs_dev // n), lambda i: (0, i, 0)),
        compiler_params=pltpu.CompilerParams(vmem_limit_bytes=40 * 1024 * 1024),
    )(scaled, polar)


def product_kernel(factor, per, resid, early, late, out):
    across = (((1,), (1,)), ((), ()))
    n_mode, n, rows, _ = resid.shape
    first = early.shape[2]
    for h in range(per):
        total = 0.0
        for d in range(n):
            block = jnp.concatenate([resid[j, d] for j in range(h, n_mode, per)], axis=1)
            for weights, cut in ((early, block[:, :first]), (late, block[:, first:])):
                total = total + lax.dot_general(
                    weights[d], cut, across, preferred_element_type=jnp.float32
                )
        out[:, h * rows : (h + 1) * rows] = total * factor


def product(resid, early, late, per, factor):
    n_mode, n, rows, width = resid.shape
    cols = early.shape[1]
    tile = tile_of(cols, 224)
    return pl.pallas_call(
        functools.partial(product_kernel, factor, per),
        grid=(cols // tile,),
        out_shape=jax.ShapeDtypeStruct((cols, per * rows), jnp.float32),
        in_specs=[
            pl.BlockSpec((n_mode, n, rows, width), lambda i: (0, 0, 0, 0)),
            pl.BlockSpec((n, tile, early.shape[2]), lambda i: (0, i, 0)),
            pl.BlockSpec((n, tile, late.shape[2]), lambda i: (0, i, 0)),
        ],
        out_specs=pl.BlockSpec((tile, per * rows), lambda i: (i, 0)),
        compiler_params=pltpu.CompilerParams(vmem_limit_bytes=56 * 1024 * 1024),
    )(resid, early, late)


def on_device(coords, curvature, weight, polar, forces):
    f32 = jnp.float32
    bf16 = jnp.bfloat16
    n_cfg, n_mode = lax.axis_size("cfg"), lax.axis_size("mode")
    per = n_mode // n_cfg
    rows, configs_dev = coords.shape
    width = configs_dev // n_cfg
    factor = 1.0 / math.sqrt(configs_dev * n_cfg)
    scaled = (coords.astype(f32) * curvature[:, None]).astype(bf16)
    weighted = (coords.astype(f32) * weight[:, None]).astype(bf16)
    part = share(scaled.T, polar, n_cfg)
    part = part.reshape(n_cfg, n_cfg, per, rows, width).transpose(0, 2, 1, 3, 4)
    part = part.reshape(n_mode * n_cfg * rows, width)
    part, weighted, forces = lax.optimization_barrier((part, weighted, forces))
    shares = lax.psum_scatter(
        part, "mode", scatter_dimension=0, tiled=True
    ).reshape(n_cfg, rows, width)
    first = configs_dev * 3 // 4
    early = exchange(weighted[:, :first], "cfg", n_cfg, 1, True, True, 0)
    pushes = exchange(
        forces.reshape(rows, n_cfg, width).transpose(1, 0, 2), "mode", n_cfg, per, False, False, 1
    )
    pushes, early = lax.optimization_barrier((pushes, early))
    mine = (pushes.astype(f32) + shares.astype(f32)).astype(bf16)
    mine = exchange(mine, "cfg", n_cfg, 1, False, True, 2)
    mine, rest = lax.optimization_barrier((mine, weighted[:, first:]))
    late = exchange(rest, "cfg", n_cfg, 1, True, True, 3)
    resid = lax.all_gather(
        mine.reshape(n_cfg * rows, width), "mode", axis=0, tiled=True
    ).reshape(n_mode, n_cfg, rows, width)
    return product(resid, early, late, per, factor).T


def solution(mesh):
    placed = (P("mode", "cfg"), P("mode"), P("mode"), P("mode", None), P("mode", "cfg"))
    return jax.shard_map(
        on_device, mesh=mesh, in_specs=placed, out_specs=P("cfg", "mode"), check_vma=False
    )
```

```python
import functools
import math

import jax
import jax.numpy as jnp
from jax import lax
from jax.experimental import pallas as pl
from jax.experimental.pallas import tpu as pltpu
from jax.sharding import PartitionSpec as P


def tile_of(extent, most):
    return max(t for t in range(8, most + 1, 8) if extent % t == 0)


def exchange_kernel(n, axis, step, whole, relative, x_ref, out_ref, send, recv, own):
    me = lax.axis_index(axis)
    here, rest = me // step, lax.rem(me, step)
    barrier = pltpu.get_barrier_semaphore()
    for d in range(1, n):
        target = lax.rem(here + d, n) * step + rest
        pl.semaphore_signal(
            barrier, inc=1, device_id={axis: target}, device_id_type=pl.DeviceIdType.MESH
        )
    pl.semaphore_wait(barrier, n - 1)
    copies = []
    for d in range(1, n):
        place = lax.rem(here + d, n)
        copies.append(
            pltpu.make_async_remote_copy(
                src_ref=x_ref if whole else x_ref.at[place],
                dst_ref=out_ref.at[n - d if relative else here],
                send_sem=send.at[d - 1],
                recv_sem=recv.at[d - 1],
                device_id={axis: place * step + rest},
                device_id_type=pl.DeviceIdType.MESH,
            )
        )
    local = pltpu.make_async_copy(
        x_ref if whole else x_ref.at[here], out_ref.at[0 if relative else here], own
    )
    for copy in copies:
        copy.start()
    local.start()
    local.wait()
    for copy in copies:
        copy.wait()


def exchange(x, axis, n, step, whole, relative, number):
    slab = x.shape if whole else x.shape[1:]
    return pl.pallas_call(
        functools.partial(exchange_kernel, n, axis, step, whole, relative),
        out_shape=jax.ShapeDtypeStruct((n, *slab), x.dtype),
        in_specs=[pl.BlockSpec(memory_space=pltpu.VMEM)],
        out_specs=pl.BlockSpec(memory_space=pl.ANY),
        scratch_shapes=[
            pltpu.SemaphoreType.DMA((n - 1,)),
            pltpu.SemaphoreType.DMA((n - 1,)),
            pltpu.SemaphoreType.DMA,
        ],
        cost_estimate=pl.CostEstimate(flops=0, bytes_accessed=150_000_000, transcendentals=0),
        compiler_params=pltpu.CompilerParams(
            collective_id=number, has_side_effects=True, vmem_limit_bytes=16 * 1024 * 1024
        ),
    )(x)


def share_kernel(scaled, polar, out):
    block = lax.dot_general(
        scaled[...], polar[...], (((1,), (0,)), ((), ())), preferred_element_type=jnp.float32
    ).astype(out.dtype)
    width = out.shape[2]
    for q in range(out.shape[0]):
        out[q] = block[q * width : (q + 1) * width].T


def share(scaled, polar, n):
    configs_dev, rows = scaled.shape
    whole = polar.shape[1]
    tile = max(t for t in range(128, 1153, 128) if whole % t == 0)
    return pl.pallas_call(
        share_kernel,
        grid=(whole // tile,),
        out_shape=jax.ShapeDtypeStruct((n, whole, configs_dev // n), polar.dtype),
        in_specs=[
            pl.BlockSpec((configs_dev, rows), lambda i: (0, 0)),
            pl.BlockSpec((rows, tile), lambda i: (0, i)),
        ],
        out_specs=pl.BlockSpec((n, tile, configs_dev // n), lambda i: (0, i, 0)),
        compiler_params=pltpu.CompilerParams(vmem_limit_bytes=40 * 1024 * 1024),
    )(scaled, polar)


def product_kernel(factor, per, resid, early, late, out):
    across = (((1,), (1,)), ((), ()))
    n_mode, n, rows, _ = resid.shape
    first = early.shape[2]
    for h in range(per):
        total = 0.0
        for d in range(n):
            block = jnp.concatenate([resid[j, d] for j in range(h, n_mode, per)], axis=1)
            for weights, cut in ((early, block[:, :first]), (late, block[:, first:])):
                total = total + lax.dot_general(
                    weights[d], cut, across, preferred_element_type=jnp.float32
                )
        out[:, h * rows : (h + 1) * rows] = total * factor


def product(resid, early, late, per, factor):
    n_mode, n, rows, width = resid.shape
    cols = early.shape[1]
    tile = tile_of(cols, 224)
    return pl.pallas_call(
        functools.partial(product_kernel, factor, per),
        grid=(cols // tile,),
        out_shape=jax.ShapeDtypeStruct((cols, per * rows), jnp.float32),
        in_specs=[
            pl.BlockSpec((n_mode, n, rows, width), lambda i: (0, 0, 0, 0)),
            pl.BlockSpec((n, tile, early.shape[2]), lambda i: (0, i, 0)),
            pl.BlockSpec((n, tile, late.shape[2]), lambda i: (0, i, 0)),
        ],
        out_specs=pl.BlockSpec((tile, per * rows), lambda i: (i, 0)),
        compiler_params=pltpu.CompilerParams(vmem_limit_bytes=56 * 1024 * 1024),
    )(resid, early, late)


def on_device(coords, curvature, weight, polar, forces):
    f32 = jnp.float32
    bf16 = jnp.bfloat16
    n_cfg, n_mode = lax.axis_size("cfg"), lax.axis_size("mode")
    per = n_mode // n_cfg
    rows, configs_dev = coords.shape
    width = configs_dev // n_cfg
    factor = 1.0 / math.sqrt(configs_dev * n_cfg)
    scaled = (coords.astype(f32) * curvature[:, None]).astype(bf16)
    weighted = (coords.astype(f32) * weight[:, None]).astype(bf16)
    part = share(scaled.T, polar, n_cfg)
    part = part.reshape(n_cfg, n_cfg, per, rows, width).transpose(0, 2, 1, 3, 4)
    part = part.reshape(n_mode * n_cfg * rows, width)
    part, weighted, forces = lax.optimization_barrier((part, weighted, forces))
    shares = lax.psum_scatter(
        part, "mode", scatter_dimension=0, tiled=True
    ).reshape(n_cfg, rows, width)
    first = configs_dev // 2
    early = exchange(weighted[:, :first], "cfg", n_cfg, 1, True, True, 0)
    pushes = exchange(
        forces.reshape(rows, n_cfg, width).transpose(1, 0, 2), "mode", n_cfg, per, False, False, 1
    )
    pushes, early = lax.optimization_barrier((pushes, early))
    mine = (pushes.astype(f32) + shares.astype(f32)).astype(bf16)
    mine = exchange(mine, "cfg", n_cfg, 1, False, True, 2)
    mine, rest = lax.optimization_barrier((mine, weighted[:, first:]))
    late = exchange(rest, "cfg", n_cfg, 1, True, True, 3)
    resid = lax.all_gather(
        mine.reshape(n_cfg * rows, width), "mode", axis=0, tiled=True
    ).reshape(n_mode, n_cfg, rows, width)
    return product(resid, early, late, per, factor).T


def solution(mesh):
    placed = (P("mode", "cfg"), P("mode"), P("mode"), P("mode", None), P("mode", "cfg"))
    return jax.shard_map(
        on_device, mesh=mesh, in_specs=placed, out_specs=P("cfg", "mode"), check_vma=False
    )
```
